32 devices in a mesh: groups: 2 (over y), ctx: 4 (over z), heads: 2 (over x), rep: 2 (over core).
Axes of the slice: x: 2, y: 2, z: 4, core: 2. Of those that a mesh axis runs over, the one named last changes fastest.
Arguments:
- queries: bfloat16 [256, 128, 128], P(('groups', 'ctx', 'rep'), 'heads'), parts along dimension 0, may hold values from -10 to 10
- cache_keys: bfloat16 [16384, 8, 128], P(('groups', 'ctx'), 'heads'), parts along dimension 0, may hold values from -10 to 10
- cache_values: bfloat16 [16384, 8, 128], P(('groups', 'ctx'), 'heads'), parts along dimension 0, may hold values from -6 to 6
- new_keys: bfloat16 [256, 8, 128], P(('groups', 'ctx', 'rep'), 'heads'), parts along dimension 0, may hold values from -6 to 6
- new_values: bfloat16 [256, 8, 128], P(('groups', 'ctx', 'rep'), 'heads'), parts along dimension 0, may hold values from -6 to 6
- positions: int32 [256], P(('groups', 'ctx', 'rep')), parts along dimension 0, may hold values from 2 to 8191
- cached_length: int32 [2], P('groups'), parts along dimension 0, may hold values from 4096 to 8192
- out_weight: bfloat16 [16384, 16384], P('heads', ('ctx', 'rep')), may hold values from -0.046875 to 0.046875
Outputs:
- mixed: bfloat16 [256, 16384], P(('groups', 'heads'), ('ctx', 'rep')), parts along dimension 0
The draws below stay inside these ranges and needn't reach their ends.
There are 2 independent parts, one for each index of `groups`. The reference program is written for one: setup_inputs(seed, part) draws one part's arguments, and reference() takes and returns one part's arrays. A program takes and returns all parts, laid end to end along the dimension named above; an argument that names none is the same for every part. Nothing has to cross between parts.
All inputs are finite; a program needn't handle non-finite values.
Results may differ from the reference program's by a relative error of at most 0.0052.
Values may be sent and summed in bfloat16 or wider, within the bound.
A program may use at most 128 MiB of HBM per device.

```python
import jax
import jax.numpy as jnp
from jax import lax

D = 16384
H = 128
KVH = 8
HD = 128
KV_DEV = 2048
NQ = 128
CTX = 8192
N_CTX = 4


def draw_queries(key, part):
    base = jnp.clip(jax.random.normal(jax.random.fold_in(key, 1), (NQ, H, HD), jnp.float32), -6.0, 6.0)
    return base.astype(jnp.bfloat16)


def draw_cache_keys(key, part):
    base = jnp.clip(jax.random.normal(jax.random.fold_in(key, 3), (CTX, KVH, HD), jnp.float32), -6.0, 6.0)
    return base.astype(jnp.bfloat16)


def plant(drawn, own_key, least, largest):
    index_at = [jax.random.randint(jax.random.fold_in(own_key, axis), (), 0, length) for axis, length in enumerate(drawn.shape)]
    widest = drawn.shape.index(max(drawn.shape))
    neighbour = index_at[:widest] + [(index_at[widest] + 1) % drawn.shape[widest]] + index_at[widest + 1:]
    return drawn.at[tuple(index_at)].set(least).at[tuple(neighbour)].set(largest)


def block_levels(own_key, dims, split, low, largest):
    factor_of = 1.0
    for dim, parts in split:
        heights = jax.random.uniform(jax.random.fold_in(jax.random.fold_in(own_key, 6), dim), (parts,), jnp.float32, low / len(split), largest / len(split))
        factor_of = factor_of * jnp.repeat(jnp.exp(heights), dims[dim] // parts).reshape((-1,) + (1,) * (len(dims) - 1 - dim))
    return factor_of


def normal_values(key, shape, scale, most, pieces=(), held_as=jnp.bfloat16):
    entries = jax.random.normal(key, shape, jnp.float32) * scale
    if len(pieces) > 0:
        entries = block_levels(key, shape, pieces, -0.22, 0.18) * entries
    return jnp.clip(entries, min=-most, max=most).astype(held_as)


def setup_inputs(seed: int = 0, part: int = 0) -> dict:
    key_of = jax.random.split(jax.random.key(seed), 9)
    own_keys = jax.random.split(jax.random.fold_in(key_of[8], part), 9)
    return {
        "queries": draw_queries(jax.random.fold_in(jax.random.fold_in(key_of[8], part), 71), part),
        "cache_keys": draw_cache_keys(jax.random.fold_in(jax.random.fold_in(key_of[8], part), 71), part),
        "cache_values": normal_values(own_keys[2], (CTX, KVH, HD), 1.0, 6.0, ((0, 4), (1, 2))),
        "new_keys": normal_values(own_keys[3], (NQ, KVH, HD), 1.0, 6.0, ((0, 8), (1, 2))),
        "new_values": normal_values(own_keys[4], (NQ, KVH, HD), 1.0, 6.0, ((0, 8), (1, 2))),
        "positions": plant(jax.random.randint(own_keys[5], (NQ,), 2, CTX), jax.random.fold_in(own_keys[5], 1), 2, CTX - 1).astype(jnp.int32),
        "cached_length": jax.random.randint(own_keys[6], (1,), CTX // 2, CTX + 1).astype(jnp.int32),
        "out_weight": normal_values(key_of[7], (H * HD, D), (H * HD) ** -0.5, 0.046875, ((0, 2), (1, 8))),
    }


NEG_FILL = -1e30


def combine(state, update):
    maxima, totals, values = state
    new_max, new_tot, new_val = update
    highest = jnp.maximum(maxima, new_max)
    keeping = jnp.exp(maxima - highest)
    taking = jnp.exp(new_max - highest)
    return highest, keeping * totals + taking * new_tot, keeping[..., None] * values + taking[..., None] * new_val


def reference(queries, cache_keys, cache_values, new_keys, new_values, positions, cached_length, out_weight):
    per_group = H // KVH
    scale_factor = HD ** -0.5
    limits = jnp.minimum(cached_length[0], positions).astype(jnp.int32)
    grouped = queries.astype(jnp.float32).reshape(NQ, KVH, per_group, HD)
    own_score = jnp.einsum('tkgd,tkd->tkg', grouped, new_keys.astype(jnp.float32), precision=lax.Precision.HIGHEST) * scale_factor
    own_values = jnp.broadcast_to(new_values.astype(jnp.float32)[:, :, None, :], (NQ, KVH, per_group, HD)).reshape(NQ, H, HD)
    start_state = (own_score.reshape(NQ, H), jnp.ones((NQ, H), jnp.float32), own_values)
    key_blocks = cache_keys.reshape(N_CTX, KV_DEV, KVH, HD)
    value_blocks = cache_values.reshape(N_CTX, KV_DEV, KVH, HD)

    def visit(state, inputs):
        block_keys, block_values, index = inputs
        scores = jnp.einsum('tkgd,jkd->tkgj', grouped, block_keys.astype(jnp.float32), precision=lax.Precision.HIGHEST) * scale_factor
        slots = index * KV_DEV + jnp.arange(KV_DEV, dtype=jnp.int32)
        visible = (slots[None, :] < limits[:, None])[:, None, None, :]
        scores = jnp.where(visible, scores, NEG_FILL)
        maxima = jnp.max(scores, axis=-1)
        weights = jnp.where(visible, jnp.exp(scores - maxima[..., None]), 0.0)
        totals = jnp.sum(weights, axis=-1)
        rounded = lax.optimization_barrier(weights.astype(jnp.bfloat16))
        output = jnp.einsum('tkgj,jkd->tkgd', rounded.astype(jnp.float32), block_values.astype(jnp.float32), precision=lax.Precision.HIGHEST)
        update = (maxima.reshape(NQ, H), totals.reshape(NQ, H), output.reshape(NQ, H, HD))
        return combine(state, update), None

    final, _ = lax.scan(visit, start_state, (key_blocks, value_blocks, jnp.arange(N_CTX, dtype=jnp.int32)))
    attended = (final[2] / final[1][..., None]).astype(jnp.bfloat16).reshape(NQ, H * HD)
    return jnp.dot(attended, out_weight, preferred_element_type=jnp.float32).astype(jnp.bfloat16)
```

```python
import functools

import jax
import jax.numpy as jnp
from jax import lax
from jax.experimental import pallas as pl
from jax.experimental.pallas import tpu as pltpu
from jax.sharding import PartitionSpec as P

MASKED = -1e30
FLOOR = -1e29
LOG2E = 1.4426950408889634
MESH = pl.DeviceIdType.MESH
NT = (((1,), (1,)), ((), ()))


def kernel(
    sizes, q_ref, lim_ref, key_ref, val_ref, nk_ref, nv_ref, w_ref, out_ref,
    qg, limg, scores, psend, precv, ssend, srecv, att, acc, xsend, xrecv, wbuf,
    q_ss, q_rs, l_ss, l_rs, p_ss, p_rs, s_ss, s_rs, a_ss, a_rs, c_ss, c_rs, x_ss, x_rs, w_sem,
):
    n_ctx, n_rep, n_heads, kv, rows, per_group, head, block = sizes
    z, r, x = lax.axis_index("ctx"), lax.axis_index("rep"), lax.axis_index("heads")
    lanes = per_group * rows
    factor = head ** (-0.5) * LOG2E
    piece = min(512, block)
    depth = per_group * head
    columns = w_ref.shape[1]
    tile = min(512, columns)
    out_rows = out_ref.shape[0]

    def w_copy(k):
        return pltpu.make_async_copy(w_ref.at[pl.ds(pl.multiple_of(k * depth, depth), depth), :], wbuf.at[k], w_sem.at[k])

    def remote(src, dst, send, recv, **where):
        return pltpu.make_async_remote_copy(
            src_ref=src, dst_ref=dst, send_sem=send, recv_sem=recv, device_id=where, device_id_type=MESH
        )

    def q_copy(k, s, way):
        return remote(qg.at[k, s], qg.at[k, s], q_ss.at[k, s, way], q_rs.at[k, s], ctx=z + 1 - 2 * way)

    def lim_copy(s, d):
        return remote(limg.at[s], limg.at[s], l_ss.at[d], l_rs.at[s], ctx=d)

    def p_copy(k, s):
        return remote(psend.at[k, s], precv.at[k, z], p_ss.at[k, s], p_rs.at[k, z], ctx=s)

    def p_arrival(k, s):
        return remote(psend.at[k, s], precv.at[k, s], p_ss.at[k, s], p_rs.at[k, s], ctx=s)

    def s_copy(k, s):
        return remote(ssend.at[k, s], srecv.at[k, z], s_ss.at[k, s], s_rs.at[k, z], ctx=s)

    def s_arrival(k, s):
        return remote(ssend.at[k, s], srecv.at[k, s], s_ss.at[k, s], s_rs.at[k, s], ctx=s)

    def a_copy(k, s, way):
        return remote(att.at[k, s, r], att.at[k, s, r], a_ss.at[k, s, way], a_rs.at[k, s], ctx=z + 1 - 2 * way)

    def c_copy(k, s, step):
        other = lax.rem(r + step, n_rep)
        return remote(att.at[k, s, r], att.at[k, s, r], c_ss.at[k, s, step - 1], c_rs.at[k, s, r], rep=other)

    def c_arrival(k, s, step):
        other = lax.rem(r + step, n_rep)
        return remote(att.at[k, s, other], att.at[k, s, other], c_ss.at[k, s, step - 1], c_rs.at[k, s, other], rep=other)

    def x_copy(t, other):
        cols = pl.ds(t * tile, tile)
        return remote(xsend.at[other, :, cols], xrecv.at[x, :, cols], x_ss.at[t, other], x_rs.at[t, x], heads=other)

    def x_arrival(t, other):
        cols = pl.ds(t * tile, tile)
        return remote(xsend.at[other, :, cols], xrecv.at[other, :, cols], x_ss.at[t, other], x_rs.at[t, other], heads=other)

    for k in range(kv):
        w_copy(k).start()

    barrier = pltpu.get_barrier_semaphore()
    for step in range(1, n_ctx):
        pl.semaphore_signal(barrier, inc=1, device_id={"ctx": lax.rem(z + step, n_ctx)}, device_id_type=MESH)
    for step in range(1, n_rep):
        pl.semaphore_signal(barrier, inc=1, device_id={"rep": lax.rem(r + step, n_rep)}, device_id_type=MESH)
    for step in range(1, n_heads):
        pl.semaphore_signal(barrier, inc=1, device_id={"heads": lax.rem(x + step, n_heads)}, device_id_type=MESH)
    qg[:, z] = q_ref[...]
    limg[z] = lim_ref[...]
    pl.semaphore_wait(barrier, n_ctx + n_rep + n_heads - 3)

    right, left = z < n_ctx - 1, z > 0

    def send_own(k):
        @pl.when(right)
        def _():
            q_copy(k, z, 0).start()

        @pl.when(left)
        def _():
            q_copy(k, z, 1).start()

    send_own(0)
    for step in range(1, n_ctx):
        lim_copy(z, lax.rem(z + step, n_ctx)).start()

    def attend(k, s):
        query = qg[k, s]
        limit = limg[s][0:1, :] - z * block
        peak = jnp.full((1, lanes), FLOOR, jnp.float32)
        for c in range(block // piece):
            span = slice(c * piece, (c + 1) * piece)
            raw = lax.dot_general(key_ref[k, span, :], query, NT, preferred_element_type=jnp.float32)
            slot = lax.broadcasted_iota(jnp.int32, (piece, lanes), 0) + c * piece
            raw = jnp.where(slot < limit, raw, MASKED)
            scores[span, :] = raw
            peak = jnp.maximum(peak, jnp.max(raw, axis=0, keepdims=True))
        total = jnp.zeros((1, lanes), jnp.float32)
        output = jnp.zeros((head, lanes), jnp.float32)
        for c in range(block // piece):
            span = slice(c * piece, (c + 1) * piece)
            weights = jnp.exp2((scores[span, :] - peak) * factor)
            total = total + jnp.sum(weights, axis=0, keepdims=True)
            output = output + jnp.dot(val_ref[k, :, span], weights.astype(jnp.bfloat16), preferred_element_type=jnp.float32)
        row = lax.broadcasted_iota(jnp.int32, (8, lanes), 0)
        stats = jnp.where(row == 0, peak, total)

        @pl.when(s == z)
        def _():
            precv[k, z] = output.astype(jnp.bfloat16)
            srecv[k, z] = stats

        @pl.when(s != z)
        def _():
            psend[k, s] = output.astype(jnp.bfloat16)
            ssend[k, s] = stats
            p_copy(k, s).start()
            s_copy(k, s).start()

    def attention(k):
        @pl.when(k + 1 < kv)
        def _():
            send_own(k + 1)

        def visit(i, carry):
            @pl.when(jnp.logical_and(i > 0, z - i >= 0))
            def _():
                q_copy(k, z - i, 0).wait_recv()

                @pl.when(right)
                def _():
                    q_copy(k, z - i, 0).start()

                @pl.when(k == 0)
                def _():
                    lim_copy(z - i, z - i).wait_recv()

            @pl.when(jnp.logical_and(i > 0, z + i < n_ctx))
            def _():
                q_copy(k, z + i, 1).wait_recv()

                @pl.when(left)
                def _():
                    q_copy(k, z + i, 1).start()

                @pl.when(k == 0)
                def _():
                    lim_copy(z + i, z + i).wait_recv()

            def side(j, inner):
                s = z - i + 2 * i * j
                real = jnp.logical_and(s >= 0, s < n_ctx)

                @pl.when(jnp.logical_and(real, jnp.logical_or(i > 0, j == 0)))
                def _():
                    attend(k, s)

                return inner

            return lax.fori_loop(0, 2, side, carry)

        lax.fori_loop(0, n_ctx, visit, 0)

    def merge(k):
        for step in range(1, n_ctx):
            s = lax.rem(z + step, n_ctx)
            p_arrival(k, s).wait_recv()
            s_arrival(k, s).wait_recv()
        query = qg[k, z]
        own_all = lax.dot_general(nk_ref[k], query, NT, preferred_element_type=jnp.float32)
        token = lax.rem(lax.broadcasted_iota(jnp.int32, (rows, lanes), 1), rows)
        same = token == lax.broadcasted_iota(jnp.int32, (rows, lanes), 0)
        own = jnp.sum(jnp.where(same, own_all, 0.0), axis=0, keepdims=True)
        own_value = jnp.dot(
            nv_ref[k], jnp.where(same, 1.0, 0.0).astype(jnp.bfloat16), preferred_element_type=jnp.float32
        )
        top = own
        for b in range(n_ctx):
            top = jnp.maximum(top, srecv[k, b, 0:1, :])
        share = jnp.exp2((own - top) * factor)
        below = share
        above = share * own_value
        for b in range(n_ctx):
            share = jnp.exp2((srecv[k, b, 0:1, :] - top) * factor)
            below = below + share * srecv[k, b, 1:2, :]
            above = above + share * precv[k, b].astype(jnp.float32)
        result = jnp.transpose(above / below).astype(jnp.bfloat16)
        for h in range(per_group):
            att[k, z, r, :, h * head : (h + 1) * head] = result[h * rows : (h + 1) * rows, :]

        @pl.when(right)
        def _():
            a_copy(k, z, 0).start()

        @pl.when(left)
        def _():
            a_copy(k, z, 1).start()

        for step in range(1, n_rep):
            c_copy(k, z, step).start()

    def collect(k):
        def hop(i, carry):
            @pl.when(z - i >= 0)
            def _():
                a_copy(k, z - i, 0).wait_recv()

                @pl.when(right)
                def _():
                    a_copy(k, z - i, 0).start()

                for step in range(1, n_rep):
                    c_copy(k, z - i, step).start()

            @pl.when(z + i < n_ctx)
            def _():
                a_copy(k, z + i, 1).wait_recv()

                @pl.when(left)
                def _():
                    a_copy(k, z + i, 1).start()

                for step in range(1, n_rep):
                    c_copy(k, z + i, step).start()

            return carry

        lax.fori_loop(1, n_ctx, hop, 0)
        for step in range(1, n_rep):
            for s in range(n_ctx):
                c_arrival(k, s, step).wait_recv()
        w_copy(k).wait()

    def product(k, t):
        cols = pl.ds(pl.multiple_of(t * tile, tile), tile)
        term = jnp.dot(
            att[k].reshape(n_ctx * n_rep * rows, depth), wbuf[k, :, cols], preferred_element_type=jnp.float32
        )
        acc[:, cols] += term

    acc[...] = jnp.zeros_like(acc)

    def stage(k, carry):
        @pl.when(k < kv)
        def _():
            attention(k)

        @pl.when(k >= 1)
        def _():
            merge(k - 1)

        @pl.when(k >= 2)
        def _():
            collect(k - 2)
            lax.fori_loop(0, columns // tile, lambda t, c: (product(k - 2, t), c)[1], 0)

        return carry

    lax.fori_loop(0, kv + 1, stage, 0)
    collect(kv - 1)
    for t in range(columns // tile):
        product(kv - 1, t)
        for other in range(n_heads):
            xsend[other, :, t * tile : (t + 1) * tile] = acc[
                other * out_rows : (other + 1) * out_rows, t * tile : (t + 1) * tile
            ].astype(jnp.bfloat16)
        for step in range(1, n_heads):
            x_copy(t, lax.rem(x + step, n_heads)).start()
    for t in range(columns // tile):
        cols = slice(t * tile, (t + 1) * tile)
        total = acc[pl.ds(pl.multiple_of(x * out_rows, out_rows), out_rows), cols]
        for step in range(1, n_heads):
            other = lax.rem(x + step, n_heads)
            x_arrival(t, other).wait_recv()
            total = total + xrecv[other, :, cols].astype(jnp.float32)
        out_ref[:, cols] = total.astype(jnp.bfloat16)

    for step in range(1, n_ctx):
        lim_copy(z, lax.rem(z + step, n_ctx)).wait_send()

    def drain(k, carry):
        def each(s, inner):
            @pl.when(s != z)
            def _():
                p_copy(k, s).wait_send()
                s_copy(k, s).wait_send()

            @pl.when(jnp.logical_and(right, s <= z))
            def _():
                q_copy(k, s, 0).wait_send()
                a_copy(k, s, 0).wait_send()

            @pl.when(jnp.logical_and(left, s >= z))
            def _():
                q_copy(k, s, 1).wait_send()
                a_copy(k, s, 1).wait_send()

            for step in range(1, n_rep):
                c_copy(k, s, step).wait_send()
            return inner

        return lax.fori_loop(0, n_ctx, each, carry)

    lax.fori_loop(0, kv, drain, 0)
    for t in range(columns // tile):
        for step in range(1, n_heads):
            x_copy(t, lax.rem(x + step, n_heads)).wait_send()


def local(mesh_shape, queries, cache_keys, cache_values, new_keys, new_values, positions, cached_length, out_weight):
    rows, local_heads, head = queries.shape
    block, kv = cache_keys.shape[0], cache_keys.shape[1]
    per_group = local_heads // kv
    n_ctx, n_rep, n_heads = mesh_shape["ctx"], mesh_shape["rep"], mesh_shape["heads"]
    lanes = per_group * rows
    depth = per_group * head
    columns = out_weight.shape[1]
    tile = min(512, columns)
    tokens = n_ctx * n_rep * rows
    out_rows = tokens // n_heads

    grouped = queries.reshape(rows, kv, per_group, head).transpose(1, 2, 0, 3).reshape(kv, lanes, head)
    limits = jnp.minimum(cached_length[0], positions)
    limits = jnp.broadcast_to(limits[None, None, :], (8, per_group, rows)).reshape(8, lanes)
    keys = cache_keys.transpose(1, 0, 2)
    values = cache_values.transpose(1, 2, 0)
    own_keys = new_keys.transpose(1, 0, 2)
    own_values = new_values.transpose(1, 2, 0)

    sizes = (n_ctx, n_rep, n_heads, kv, rows, per_group, head, block)
    dma = pltpu.SemaphoreType.DMA
    vmem = pl.BlockSpec(memory_space=pltpu.VMEM)
    return pl.pallas_call(
        functools.partial(kernel, sizes),
        out_shape=jax.ShapeDtypeStruct((out_rows, columns), jnp.bfloat16),
        in_specs=[vmem] * 6 + [pl.BlockSpec(memory_space=pl.ANY)],
        out_specs=vmem,
        scratch_shapes=[
            pltpu.VMEM((kv, n_ctx, lanes, head), jnp.bfloat16),
            pltpu.VMEM((n_ctx, 8, lanes), jnp.int32),
            pltpu.VMEM((block, lanes), jnp.float32),
            pltpu.VMEM((kv, n_ctx, head, lanes), jnp.bfloat16),
            pltpu.VMEM((kv, n_ctx, head, lanes), jnp.bfloat16),
            pltpu.VMEM((kv, n_ctx, 8, lanes), jnp.float32),
            pltpu.VMEM((kv, n_ctx, 8, lanes), jnp.float32),
            pltpu.VMEM((kv, n_ctx, n_rep, rows, depth), jnp.bfloat16),
            pltpu.VMEM((tokens, columns), jnp.float32),
            pltpu.VMEM((n_heads, out_rows, columns), jnp.bfloat16),
            pltpu.VMEM((n_heads, out_rows, columns), jnp.bfloat16),
            pltpu.VMEM((kv, depth, columns), jnp.bfloat16),
            dma((kv, n_ctx, 2)),
            dma((kv, n_ctx)),
            dma((n_ctx,)),
            dma((n_ctx,)),
            dma((kv, n_ctx)),
            dma((kv, n_ctx)),
            dma((kv, n_ctx)),
            dma((kv, n_ctx)),
            dma((kv, n_ctx, 2)),
            dma((kv, n_ctx)),
            dma((kv, n_ctx, n_rep)),
            dma((kv, n_ctx, n_rep)),
            dma((columns // tile, n_heads)),
            dma((columns // tile, n_heads)),
            dma((kv,)),
        ],
        compiler_params=pltpu.CompilerParams(
            collective_id=0, has_side_effects=True, vmem_limit_bytes=60 * 1024 * 1024
        ),
    )(grouped, limits, keys, values, own_keys, own_values, out_weight)


def solution(mesh):
    return jax.shard_map(
        functools.partial(local, dict(mesh.shape)),
        mesh=mesh,
        in_specs=(
            P(("groups", "ctx", "rep"), "heads", None),
            P(("groups", "ctx"), "heads", None),
            P(("groups", "ctx"), "heads", None),
            P(("groups", "ctx", "rep"), "heads", None),
            P(("groups", "ctx", "rep"), "heads", None),
            P(("groups", "ctx", "rep")),
            P("groups"),
            P("heads", ("ctx", "rep")),
        ),
        out_specs=P(("groups", "heads"), ("ctx", "rep")),
        check_vma=False,
    )
```

```python
import functools

import jax
import jax.numpy as jnp
from jax import lax
from jax.experimental import pallas as pl
from jax.experimental.pallas import tpu as pltpu
from jax.sharding import PartitionSpec as P

MASKED = -1e30
FLOOR = -1e29
LOG2E = 1.4426950408889634
MESH = pl.DeviceIdType.MESH
NT = (((1,), (1,)), ((), ()))


def kernel(
    sizes, pos_ref, len_ref, q_ref, ck_ref, cv_ref, nk_ref, nv_ref, w_ref, out_ref,
    wide, kraw, vraw, key_ref, val_ref, qg, limg, scores, psend, precv, ssend, srecv, att, acc, xsend, xrecv, wbuf,
    q_ss, q_rs, l_ss, l_rs, p_ss, p_rs, s_ss, s_rs, a_ss, a_rs, c_ss, c_rs, x_ss, x_rs, w_sem, kv_sem,
):
    n_ctx, n_rep, n_heads, kv, rows, per_group, head, block = sizes
    z, r, x = lax.axis_index("ctx"), lax.axis_index("rep"), lax.axis_index("heads")
    lanes = per_group * rows
    factor = head ** (-0.5) * LOG2E
    piece = min(512, block)
    depth = per_group * head
    columns = w_ref.shape[1]
    tile = min(512, columns)
    out_rows = out_ref.shape[0]

    def w_copy(k):
        return pltpu.make_async_copy(w_ref.at[pl.ds(pl.multiple_of(k * depth, depth), depth), :], wbuf.at[k], w_sem.at[k])

    def remote(src, dst, send, recv, **where):
        return pltpu.make_async_remote_copy(
            src_ref=src, dst_ref=dst, send_sem=send, recv_sem=recv, device_id=where, device_id_type=MESH
        )

    def q_copy(k, s, way):
        return remote(qg.at[k, s], qg.at[k, s], q_ss.at[k, s, way], q_rs.at[k, s], ctx=z + 1 - 2 * way)

    def lim_copy(s, d):
        return remote(limg.at[s], limg.at[s], l_ss.at[d], l_rs.at[s], ctx=d)

    def p_copy(k, s):
        return remote(psend.at[k, s], precv.at[k, z], p_ss.at[k, s], p_rs.at[k, z], ctx=s)

    def p_arrival(k, s):
        return remote(psend.at[k, s], precv.at[k, s], p_ss.at[k, s], p_rs.at[k, s], ctx=s)

    def s_copy(k, s):
        return remote(ssend.at[k, s], srecv.at[k, z], s_ss.at[k, s], s_rs.at[k, z], ctx=s)

    def s_arrival(k, s):
        return remote(ssend.at[k, s], srecv.at[k, s], s_ss.at[k, s], s_rs.at[k, s], ctx=s)

    def a_copy(k, s, way):
        return remote(att.at[k, s, r], att.at[k, s, r], a_ss.at[k, s, way], a_rs.at[k, s], ctx=z + 1 - 2 * way)

    def c_copy(k, s, step):
        other = lax.rem(r + step, n_rep)
        return remote(att.at[k, s, r], att.at[k, s, r], c_ss.at[k, s, step - 1], c_rs.at[k, s, r], rep=other)

    def c_arrival(k, s, step):
        other = lax.rem(r + step, n_rep)
        return remote(att.at[k, s, other], att.at[k, s, other], c_ss.at[k, s, step - 1], c_rs.at[k, s, other], rep=other)

    def x_copy(t, other):
        cols = pl.ds(t * tile, tile)
        return remote(xsend.at[other, :, cols], xrecv.at[x, :, cols], x_ss.at[t, other], x_rs.at[t, x], heads=other)

    def x_arrival(t, other):
        cols = pl.ds(t * tile, tile)
        return remote(xsend.at[other, :, cols], xrecv.at[other, :, cols], x_ss.at[t, other], x_rs.at[t, other], heads=other)

    k_copy = pltpu.make_async_copy(ck_ref, kraw, kv_sem.at[0])
    v_copy = pltpu.make_async_copy(cv_ref, vraw, kv_sem.at[1])
    k_copy.start()
    v_copy.start()
    for k in range(kv):
        w_copy(k).start()

    barrier = pltpu.get_barrier_semaphore()
    for step in range(1, n_ctx):
        pl.semaphore_signal(barrier, inc=1, device_id={"ctx": lax.rem(z + step, n_ctx)}, device_id_type=MESH)
    for step in range(1, n_rep):
        pl.semaphore_signal(barrier, inc=1, device_id={"rep": lax.rem(r + step, n_rep)}, device_id_type=MESH)
    for step in range(1, n_heads):
        pl.semaphore_signal(barrier, inc=1, device_id={"heads": lax.rem(x + step, n_heads)}, device_id_type=MESH)
    heads_here = kv * per_group
    wide[: rows * heads_here, :] = q_ref[...].astype(jnp.float32)
    for k in range(kv):
        for h in range(per_group):
            picked = wide[pl.ds(k * per_group + h, rows, stride=heads_here), :]
            qg[k, z, h * rows : (h + 1) * rows, :] = picked.astype(jnp.bfloat16)
    lane_token = lax.rem(lax.broadcasted_iota(jnp.int32, (8, lanes), 1), rows)
    limit_row = jnp.zeros((8, lanes), jnp.int32)
    for t in range(rows):
        limit_row = jnp.where(lane_token == t, jnp.minimum(len_ref[0], pos_ref[t]), limit_row)
    limg[z] = limit_row
    pl.semaphore_wait(barrier, n_ctx + n_rep + n_heads - 3)

    right, left = z < n_ctx - 1, z > 0

    def send_own(k):
        @pl.when(right)
        def _():
            q_copy(k, z, 0).start()

        @pl.when(left)
        def _():
            q_copy(k, z, 1).start()

    send_own(0)
    for step in range(1, n_ctx):
        lim_copy(z, lax.rem(z + step, n_ctx)).start()

    batch = min(256, block)

    def unpack(c, carry):
        source = pl.ds(pl.multiple_of(c * batch * kv, batch * kv), batch * kv)
        span = pl.ds(pl.multiple_of(c * batch, batch), batch)
        wide[: batch * kv, :] = kraw[source, :].astype(jnp.float32)
        for k in range(kv):
            key_ref[k, span, :] = wide[pl.ds(k, batch, stride=kv), :].astype(jnp.bfloat16)
        return carry

    def unpack_values(c, carry):
        source = pl.ds(pl.multiple_of(c * batch * kv, batch * kv), batch * kv)
        span = pl.ds(pl.multiple_of(c * batch, batch), batch)
        wide[: batch * kv, :] = vraw[source, :].astype(jnp.float32)
        for k in range(kv):
            val_ref[k, :, span] = jnp.transpose(wide[pl.ds(k, batch, stride=kv), :]).astype(jnp.bfloat16)
        return carry

    k_copy.wait()
    lax.fori_loop(0, block // batch, unpack, 0)
    v_copy.wait()
    lax.fori_loop(0, block // batch, unpack_values, 0)

    def attend(k, s):
        query = qg[k, s]
        limit = limg[s][0:1, :] - z * block
        peak = jnp.full((1, lanes), FLOOR, jnp.float32)
        for c in range(block // piece):
            span = slice(c * piece, (c + 1) * piece)
            raw = lax.dot_general(key_ref[k, span, :], query, NT, preferred_element_type=jnp.float32)
            slot = lax.broadcasted_iota(jnp.int32, (piece, lanes), 0) + c * piece
            raw = jnp.where(slot < limit, raw, MASKED)
            scores[span, :] = raw
            peak = jnp.maximum(peak, jnp.max(raw, axis=0, keepdims=True))
        total = jnp.zeros((1, lanes), jnp.float32)
        output = jnp.zeros((head, lanes), jnp.float32)
        for c in range(block // piece):
            span = slice(c * piece, (c + 1) * piece)
            weights = jnp.exp2((scores[span, :] - peak) * factor)
            total = total + jnp.sum(weights, axis=0, keepdims=True)
            output = output + jnp.dot(val_ref[k, :, span], weights.astype(jnp.bfloat16), preferred_element_type=jnp.float32)
        row = lax.broadcasted_iota(jnp.int32, (8, lanes), 0)
        stats = jnp.where(row == 0, peak, total)

        @pl.when(s == z)
        def _():
            precv[k, z] = output.astype(jnp.bfloat16)
            srecv[k, z] = stats

        @pl.when(s != z)
        def _():
            psend[k, s] = output.astype(jnp.bfloat16)
            ssend[k, s] = stats
            p_copy(k, s).start()
            s_copy(k, s).start()

    def attention(k):
        @pl.when(k + 1 < kv)
        def _():
            send_own(k + 1)

        def visit(i, carry):
            @pl.when(jnp.logical_and(i > 0, z - i >= 0))
            def _():
                q_copy(k, z - i, 0).wait_recv()

                @pl.when(right)
                def _():
                    q_copy(k, z - i, 0).start()

                @pl.when(k == 0)
                def _():
                    lim_copy(z - i, z - i).wait_recv()

            @pl.when(jnp.logical_and(i > 0, z + i < n_ctx))
            def _():
                q_copy(k, z + i, 1).wait_recv()

                @pl.when(left)
                def _():
                    q_copy(k, z + i, 1).start()

                @pl.when(k == 0)
                def _():
                    lim_copy(z + i, z + i).wait_recv()

            def side(j, inner):
                s = z - i + 2 * i * j
                real = jnp.logical_and(s >= 0, s < n_ctx)

                @pl.when(jnp.logical_and(real, jnp.logical_or(i > 0, j == 0)))
                def _():
                    attend(k, s)

                return inner

            return lax.fori_loop(0, 2, side, carry)

        lax.fori_loop(0, n_ctx, visit, 0)

    def merge(k):
        for step in range(1, n_ctx):
            s = lax.rem(z + step, n_ctx)
            p_arrival(k, s).wait_recv()
            s_arrival(k, s).wait_recv()
        query = qg[k, z]
        wide[: rows * kv, :] = nk_ref[...].astype(jnp.float32)
        own_key = wide[pl.ds(k, rows, stride=kv), :].astype(jnp.bfloat16)
        own_all = lax.dot_general(own_key, query, NT, preferred_element_type=jnp.float32)
        token = lax.rem(lax.broadcasted_iota(jnp.int32, (rows, lanes), 1), rows)
        same = token == lax.broadcasted_iota(jnp.int32, (rows, lanes), 0)
        own = jnp.sum(jnp.where(same, own_all, 0.0), axis=0, keepdims=True)
        wide[: rows * kv, :] = nv_ref[...].astype(jnp.float32)
        own_value = lax.dot_general(
            wide[pl.ds(k, rows, stride=kv), :].astype(jnp.bfloat16),
            jnp.where(same, 1.0, 0.0).astype(jnp.bfloat16),
            (((0,), (0,)), ((), ())),
            preferred_element_type=jnp.float32,
        )
        top = own
        for b in range(n_ctx):
            top = jnp.maximum(top, srecv[k, b, 0:1, :])
        share = jnp.exp2((own - top) * factor)
        below = share
        above = share * own_value
        for b in range(n_ctx):
            share = jnp.exp2((srecv[k, b, 0:1, :] - top) * factor)
            below = below + share * srecv[k, b, 1:2, :]
            above = above + share * precv[k, b].astype(jnp.float32)
        result = jnp.transpose(above / below).astype(jnp.bfloat16)
        for h in range(per_group):
            att[k, z, r, :, h * head : (h + 1) * head] = result[h * rows : (h + 1) * rows, :]

        @pl.when(right)
        def _():
            a_copy(k, z, 0).start()

        @pl.when(left)
        def _():
            a_copy(k, z, 1).start()

        for step in range(1, n_rep):
            c_copy(k, z, step).start()

    def collect(k):
        def hop(i, carry):
            @pl.when(z - i >= 0)
            def _():
                a_copy(k, z - i, 0).wait_recv()

                @pl.when(right)
                def _():
                    a_copy(k, z - i, 0).start()

                for step in range(1, n_rep):
                    c_copy(k, z - i, step).start()

            @pl.when(z + i < n_ctx)
            def _():
                a_copy(k, z + i, 1).wait_recv()

                @pl.when(left)
                def _():
                    a_copy(k, z + i, 1).start()

                for step in range(1, n_rep):
                    c_copy(k, z + i, step).start()

            return carry

        lax.fori_loop(1, n_ctx, hop, 0)
        for step in range(1, n_rep):
            for s in range(n_ctx):
                c_arrival(k, s, step).wait_recv()
        w_copy(k).wait()

    def product(k, t):
        cols = pl.ds(pl.multiple_of(t * tile, tile), tile)
        term = jnp.dot(
            att[k].reshape(n_ctx * n_rep * rows, depth), wbuf[k, :, cols], preferred_element_type=jnp.float32
        )
        acc[:, cols] += term

    acc[...] = jnp.zeros_like(acc)

    def stage(k, carry):
        @pl.when(k < kv)
        def _():
            attention(k)

        @pl.when(k >= 1)
        def _():
            merge(k - 1)

        @pl.when(k >= 2)
        def _():
            collect(k - 2)
            lax.fori_loop(0, columns // tile, lambda t, c: (product(k - 2, t), c)[1], 0)

        return carry

    lax.fori_loop(0, kv + 1, stage, 0)
    collect(kv - 1)
    for t in range(columns // tile):
        product(kv - 1, t)
        for other in range(n_heads):
            xsend[other, :, t * tile : (t + 1) * tile] = acc[
                other * out_rows : (other + 1) * out_rows, t * tile : (t + 1) * tile
            ].astype(jnp.bfloat16)
        for step in range(1, n_heads):
            x_copy(t, lax.rem(x + step, n_heads)).start()
    for t in range(columns // tile):
        cols = slice(t * tile, (t + 1) * tile)
        total = acc[pl.ds(pl.multiple_of(x * out_rows, out_rows), out_rows), cols]
        for step in range(1, n_heads):
            other = lax.rem(x + step, n_heads)
            x_arrival(t, other).wait_recv()
            total = total + xrecv[other, :, cols].astype(jnp.float32)
        out_ref[:, cols] = total.astype(jnp.bfloat16)

    for step in range(1, n_ctx):
        lim_copy(z, lax.rem(z + step, n_ctx)).wait_send()

    def drain(k, carry):
        def each(s, inner):
            @pl.when(s != z)
            def _():
                p_copy(k, s).wait_send()
                s_copy(k, s).wait_send()

            @pl.when(jnp.logical_and(right, s <= z))
            def _():
                q_copy(k, s, 0).wait_send()
                a_copy(k, s, 0).wait_send()

            @pl.when(jnp.logical_and(left, s >= z))
            def _():
                q_copy(k, s, 1).wait_send()
                a_copy(k, s, 1).wait_send()

            for step in range(1, n_rep):
                c_copy(k, s, step).wait_send()
            return inner

        return lax.fori_loop(0, n_ctx, each, carry)

    lax.fori_loop(0, kv, drain, 0)
    for t in range(columns // tile):
        for step in range(1, n_heads):
            x_copy(t, lax.rem(x + step, n_heads)).wait_send()


def local(mesh_shape, queries, cache_keys, cache_values, new_keys, new_values, positions, cached_length, out_weight):
    rows, local_heads, head = queries.shape
    block, kv = cache_keys.shape[0], cache_keys.shape[1]
    per_group = local_heads // kv
    n_ctx, n_rep, n_heads = mesh_shape["ctx"], mesh_shape["rep"], mesh_shape["heads"]
    lanes = per_group * rows
    depth = per_group * head
    columns = out_weight.shape[1]
    tile = min(512, columns)
    tokens = n_ctx * n_rep * rows
    out_rows = tokens // n_heads

    sizes = (n_ctx, n_rep, n_heads, kv, rows, per_group, head, block)
    dma = pltpu.SemaphoreType.DMA
    vmem = pl.BlockSpec(memory_space=pltpu.VMEM)
    smem = pl.BlockSpec(memory_space=pltpu.SMEM)
    anywhere = pl.BlockSpec(memory_space=pl.ANY)
    return pl.pallas_call(
        functools.partial(kernel, sizes),
        out_shape=jax.ShapeDtypeStruct((out_rows, columns), jnp.bfloat16),
        in_specs=[smem, smem, vmem, anywhere, anywhere, vmem, vmem, anywhere],
        out_specs=vmem,
        scratch_shapes=[
            pltpu.VMEM((max(rows * local_heads, min(256, block) * kv), head), jnp.float32),
            pltpu.VMEM((block * kv, head), jnp.bfloat16),
            pltpu.VMEM((block * kv, head), jnp.bfloat16),
            pltpu.VMEM((kv, block, head), jnp.bfloat16),
            pltpu.VMEM((kv, head, block), jnp.bfloat16),
            pltpu.VMEM((kv, n_ctx, lanes, head), jnp.bfloat16),
            pltpu.VMEM((n_ctx, 8, lanes), jnp.int32),
            pltpu.VMEM((block, lanes), jnp.float32),
            pltpu.VMEM((kv, n_ctx, head, lanes), jnp.bfloat16),
            pltpu.VMEM((kv, n_ctx, head, lanes), jnp.bfloat16),
            pltpu.VMEM((kv, n_ctx, 8, lanes), jnp.float32),
            pltpu.VMEM((kv, n_ctx, 8, lanes), jnp.float32),
            pltpu.VMEM((kv, n_ctx, n_rep, rows, depth), jnp.bfloat16),
            pltpu.VMEM((tokens, columns), jnp.float32),
            pltpu.VMEM((n_heads, out_rows, columns), jnp.bfloat16),
            pltpu.VMEM((n_heads, out_rows, columns), jnp.bfloat16),
            pltpu.VMEM((kv, depth, columns), jnp.bfloat16),
            dma((kv, n_ctx, 2)),
            dma((kv, n_ctx)),
            dma((n_ctx,)),
            dma((n_ctx,)),
            dma((kv, n_ctx)),
            dma((kv, n_ctx)),
            dma((kv, n_ctx)),
            dma((kv, n_ctx)),
            dma((kv, n_ctx, 2)),
            dma((kv, n_ctx)),
            dma((kv, n_ctx, n_rep)),
            dma((kv, n_ctx, n_rep)),
            dma((columns // tile, n_heads)),
            dma((columns // tile, n_heads)),
            dma((kv,)),
            dma((2,)),
        ],
        compiler_params=pltpu.CompilerParams(
            collective_id=0, has_side_effects=True, vmem_limit_bytes=60 * 1024 * 1024
        ),
    )(
        positions,
        cached_length,
        queries.reshape(rows * local_heads, head),
        cache_keys.reshape(block * kv, head),
        cache_values.reshape(block * kv, head),
        new_keys.reshape(rows * kv, head),
        new_values.reshape(rows * kv, head),
        out_weight,
    )


def solution(mesh):
    return jax.shard_map(
        functools.partial(local, dict(mesh.shape)),
        mesh=mesh,
        in_specs=(
            P(("groups", "ctx", "rep"), "heads", None),
            P(("groups", "ctx"), "heads", None),
            P(("groups", "ctx"), "heads", None),
            P(("groups", "ctx", "rep"), "heads", None),
            P(("groups", "ctx", "rep"), "heads", None),
            P(("groups", "ctx", "rep")),
            P("groups"),
            P("heads", ("ctx", "rep")),
        ),
        out_specs=P(("groups", "heads"), ("ctx", "rep")),
        check_vma=False,
    )
```

```python
import functools

import jax
import jax.numpy as jnp
from jax import lax
from jax.experimental import pallas as pl
from jax.experimental.pallas import tpu as pltpu
from jax.sharding import PartitionSpec as P

MASKED = -1e30
FLOOR = -1e29
LOG2E = 1.4426950408889634
MESH = pl.DeviceIdType.MESH
NT = (((1,), (1,)), ((), ()))


def kernel(
    sizes, pos_ref, len_ref, q_ref, ck_ref, cv_ref, nk_ref, nv_ref, w_ref, out_ref,
    wide, kraw, vraw, key_ref, val_ref, qg, limg, scores, psend, precv, ssend, srecv, att, acc, xsend, xrecv, wbuf,
    q_ss, q_rs, l_ss, l_rs, p_ss, p_rs, s_ss, s_rs, a_ss, a_rs, c_ss, c_rs, x_ss, x_rs, w_sem, kv_sem,
):
    n_ctx, n_rep, n_heads, kv, rows, per_group, head, block = sizes
    z, r, x = lax.axis_index("ctx"), lax.axis_index("rep"), lax.axis_index("heads")
    lanes = per_group * rows
    factor = head ** (-0.5) * LOG2E
    piece = min(512, block)
    depth = per_group * head
    columns = w_ref.shape[1]
    tile = min(512, columns)
    out_rows = out_ref.shape[0]

    def w_copy(k):
        return pltpu.make_async_copy(w_ref.at[pl.ds(pl.multiple_of(k * depth, depth), depth), :], wbuf.at[k], w_sem.at[k])

    def remote(src, dst, send, recv, **where):
        return pltpu.make_async_remote_copy(
            src_ref=src, dst_ref=dst, send_sem=send, recv_sem=recv, device_id=where, device_id_type=MESH
        )

    def q_copy(k, s, way):
        return remote(qg.at[k, s], qg.at[k, s], q_ss.at[k, s, way], q_rs.at[k, s], ctx=z + 1 - 2 * way)

    def lim_copy(s, d):
        return remote(limg.at[s], limg.at[s], l_ss.at[d], l_rs.at[s], ctx=d)

    def p_copy(k, s):
        return remote(psend.at[k, s], precv.at[k, z], p_ss.at[k, s], p_rs.at[k, z], ctx=s)

    def p_arrival(k, s):
        return remote(psend.at[k, s], precv.at[k, s], p_ss.at[k, s], p_rs.at[k, s], ctx=s)

    def s_copy(k, s):
        return remote(ssend.at[k, s], srecv.at[k, z], s_ss.at[k, s], s_rs.at[k, z], ctx=s)

    def s_arrival(k, s):
        return remote(ssend.at[k, s], srecv.at[k, s], s_ss.at[k, s], s_rs.at[k, s], ctx=s)

    def a_copy(k, s, way):
        return remote(att.at[k, s, r], att.at[k, s, r], a_ss.at[k, s, way], a_rs.at[k, s], ctx=z + 1 - 2 * way)

    def c_copy(k, s, step):
        other = lax.rem(r + step, n_rep)
        return remote(att.at[k, s, r], att.at[k, s, r], c_ss.at[k, s, step - 1], c_rs.at[k, s, r], rep=other)

    def c_arrival(k, s, step):
        other = lax.rem(r + step, n_rep)
        return remote(att.at[k, s, other], att.at[k, s, other], c_ss.at[k, s, step - 1], c_rs.at[k, s, other], rep=other)

    def x_copy(t, other):
        cols = pl.ds(t * tile, tile)
        return remote(xsend.at[other, :, cols], xrecv.at[x, :, cols], x_ss.at[t, other], x_rs.at[t, x], heads=other)

    def x_arrival(t, other):
        cols = pl.ds(t * tile, tile)
        return remote(xsend.at[other, :, cols], xrecv.at[other, :, cols], x_ss.at[t, other], x_rs.at[t, other], heads=other)

    k_copy = pltpu.make_async_copy(ck_ref, kraw, kv_sem.at[0])
    v_copy = pltpu.make_async_copy(cv_ref, vraw, kv_sem.at[1])
    k_copy.start()
    v_copy.start()
    for k in range(kv):
        w_copy(k).start()

    barrier = pltpu.get_barrier_semaphore()
    for step in range(1, n_ctx):
        pl.semaphore_signal(barrier, inc=1, device_id={"ctx": lax.rem(z + step, n_ctx)}, device_id_type=MESH)
    for step in range(1, n_rep):
        pl.semaphore_signal(barrier, inc=1, device_id={"rep": lax.rem(r + step, n_rep)}, device_id_type=MESH)
    for step in range(1, n_heads):
        pl.semaphore_signal(barrier, inc=1, device_id={"heads": lax.rem(x + step, n_heads)}, device_id_type=MESH)
    heads_here = kv * per_group
    wide[: rows * heads_here, :] = q_ref[...].astype(jnp.float32)
    for k in range(kv):
        for h in range(per_group):
            picked = wide[pl.ds(k * per_group + h, rows, stride=heads_here), :]
            qg[k, z, h * rows : (h + 1) * rows, :] = picked.astype(jnp.bfloat16)
    lane_token = lax.rem(lax.broadcasted_iota(jnp.int32, (1, lanes), 1), rows)
    limit_row = jnp.zeros((1, lanes), jnp.int32)
    for t in range(rows):
        limit_row = jnp.where(lane_token == t, jnp.minimum(len_ref[0], pos_ref[t]), limit_row)
    limg[z] = limit_row
    pl.semaphore_wait(barrier, n_ctx + n_rep + n_heads - 3)

    right, left = z < n_ctx - 1, z > 0

    def send_own(k):
        @pl.when(right)
        def _():
            q_copy(k, z, 0).start()

        @pl.when(left)
        def _():
            q_copy(k, z, 1).start()

    for k in range(min(2, kv)):
        send_own(k)
    for step in range(1, n_ctx):
        lim_copy(z, lax.rem(z + step, n_ctx)).start()

    batch = min(256, block)

    def unpack(c, carry):
        source = pl.ds(pl.multiple_of(c * batch * kv, batch * kv), batch * kv)
        span = pl.ds(pl.multiple_of(c * batch, batch), batch)
        wide[: batch * kv, :] = kraw[source, :].astype(jnp.float32)
        for k in range(kv):
            key_ref[k, span, :] = wide[pl.ds(k, batch, stride=kv), :].astype(jnp.bfloat16)
        return carry

    def unpack_values(c, carry):
        source = pl.ds(pl.multiple_of(c * batch * kv, batch * kv), batch * kv)
        span = pl.ds(pl.multiple_of(c * batch, batch), batch)
        wide[: batch * kv, :] = vraw[source, :].astype(jnp.float32)
        for k in range(kv):
            val_ref[k, :, span] = jnp.transpose(wide[pl.ds(k, batch, stride=kv), :]).astype(jnp.bfloat16)
        return carry

    k_copy.wait()
    lax.fori_loop(0, block // batch, unpack, 0)
    v_copy.wait()
    lax.fori_loop(0, block // batch, unpack_values, 0)

    def attend(k, s):
        query = qg[k, s]
        limit = limg[s] - z * block
        peak = jnp.full((1, lanes), FLOOR, jnp.float32)
        for c in range(block // piece):
            span = slice(c * piece, (c + 1) * piece)
            raw = lax.dot_general(key_ref[k, span, :], query, NT, preferred_element_type=jnp.float32)
            slot = lax.broadcasted_iota(jnp.int32, (piece, lanes), 0) + c * piece
            raw = jnp.where(slot < limit, raw, MASKED)
            scores[span, :] = raw
            peak = jnp.maximum(peak, jnp.max(raw, axis=0, keepdims=True))
        total = jnp.zeros((1, lanes), jnp.float32)
        output = jnp.zeros((head, lanes), jnp.float32)
        for c in range(block // piece):
            span = slice(c * piece, (c + 1) * piece)
            weights = jnp.exp2((scores[span, :] - peak) * factor)
            total = total + jnp.sum(weights, axis=0, keepdims=True)
            output = output + jnp.dot(val_ref[k, :, span], weights.astype(jnp.bfloat16), preferred_element_type=jnp.float32)

        @pl.when(s == z)
        def _():
            precv[k, z] = output.astype(jnp.bfloat16)
            srecv[k, z, 0:1, :] = peak
            srecv[k, z, 1:2, :] = total

        @pl.when(s != z)
        def _():
            psend[k, s] = output.astype(jnp.bfloat16)
            ssend[k, s, 0:1, :] = peak
            ssend[k, s, 1:2, :] = total
            p_copy(k, s).start()
            s_copy(k, s).start()

    def q_hop(k, i):
        @pl.when(z - i >= 0)
        def _():
            q_copy(k, z - i, 0).wait_recv()

            @pl.when(right)
            def _():
                q_copy(k, z - i, 0).start()

            @pl.when(k == 0)
            def _():
                lim_copy(z - i, z - i).wait_recv()

        @pl.when(z + i < n_ctx)
        def _():
            q_copy(k, z + i, 1).wait_recv()

            @pl.when(left)
            def _():
                q_copy(k, z + i, 1).start()

            @pl.when(k == 0)
            def _():
                lim_copy(z + i, z + i).wait_recv()

    def visit(k, i):
        def side(j, inner):
            s = z - i + 2 * i * j
            real = jnp.logical_and(s >= 0, s < n_ctx)

            @pl.when(jnp.logical_and(real, jnp.logical_or(i > 0, j == 0)))
            def _():
                attend(k, s)

            return inner

        lax.fori_loop(0, 2, side, 0)

    def merge(k):
        for step in range(1, n_ctx):
            s = lax.rem(z + step, n_ctx)
            p_arrival(k, s).wait_recv()
            s_arrival(k, s).wait_recv()
        query = qg[k, z]
        wide[: rows * kv, :] = nk_ref[...].astype(jnp.float32)
        own_key = wide[pl.ds(k, rows, stride=kv), :].astype(jnp.bfloat16)
        own_all = lax.dot_general(own_key, query, NT, preferred_element_type=jnp.float32)
        token = lax.rem(lax.broadcasted_iota(jnp.int32, (rows, lanes), 1), rows)
        same = token == lax.broadcasted_iota(jnp.int32, (rows, lanes), 0)
        own = jnp.sum(jnp.where(same, own_all, 0.0), axis=0, keepdims=True)
        wide[: rows * kv, :] = nv_ref[...].astype(jnp.float32)
        own_value = lax.dot_general(
            wide[pl.ds(k, rows, stride=kv), :].astype(jnp.bfloat16),
            jnp.where(same, 1.0, 0.0).astype(jnp.bfloat16),
            (((0,), (0,)), ((), ())),
            preferred_element_type=jnp.float32,
        )
        top = own
        for b in range(n_ctx):
            top = jnp.maximum(top, srecv[k, b, 0:1, :])
        share = jnp.exp2((own - top) * factor)
        below = share
        above = share * own_value
        for b in range(n_ctx):
            share = jnp.exp2((srecv[k, b, 0:1, :] - top) * factor)
            below = below + share * srecv[k, b, 1:2, :]
            above = above + share * precv[k, b].astype(jnp.float32)
        result = jnp.transpose(above / below).astype(jnp.bfloat16)
        for h in range(per_group):
            att[k, z, r, :, h * head : (h + 1) * head] = result[h * rows : (h + 1) * rows, :]

        @pl.when(right)
        def _():
            a_copy(k, z, 0).start()

        @pl.when(left)
        def _():
            a_copy(k, z, 1).start()

        for step in range(1, n_rep):
            c_copy(k, z, step).start()

    def a_hop(k, i):
        @pl.when(z - i >= 0)
        def _():
            a_copy(k, z - i, 0).wait_recv()

            @pl.when(right)
            def _():
                a_copy(k, z - i, 0).start()

            for step in range(1, n_rep):
                c_copy(k, z - i, step).start()

        @pl.when(z + i < n_ctx)
        def _():
            a_copy(k, z + i, 1).wait_recv()

            @pl.when(left)
            def _():
                a_copy(k, z + i, 1).start()

            for step in range(1, n_rep):
                c_copy(k, z + i, step).start()

    def gathered(k):
        for step in range(1, n_rep):
            for s in range(n_ctx):
                c_arrival(k, s, step).wait_recv()
        w_copy(k).wait()

    def product(k, t):
        cols = pl.ds(pl.multiple_of(t * tile, tile), tile)
        term = jnp.dot(
            att[k].reshape(n_ctx * n_rep * rows, depth), wbuf[k, :, cols], preferred_element_type=jnp.float32
        )
        acc[:, cols] += term

    acc[...] = jnp.zeros_like(acc)

    def stage(k, carry):
        @pl.when(k + 2 < kv)
        def _():
            send_own(k + 2)

        def step_of(i, inner):
            @pl.when(jnp.logical_and(k < kv, i > 0))
            def _():
                q_hop(k, i)

            @pl.when(jnp.logical_and(k >= 2, i > 0))
            def _():
                a_hop(k - 2, i)

            @pl.when(jnp.logical_and(jnp.logical_and(k >= 1, k <= kv), i == n_ctx // 2))
            def _():
                merge(k - 1)

            @pl.when(k < kv)
            def _():
                visit(k, i)

            return inner

        lax.fori_loop(0, n_ctx, step_of, 0)

        @pl.when(k >= 2)
        def _():
            gathered(k - 2)

        @pl.when(jnp.logical_and(k >= 2, k <= kv))
        def _():
            lax.fori_loop(0, columns // tile, lambda t, c: (product(k - 2, t), c)[1], 0)

        return carry

    lax.fori_loop(0, kv + 2, stage, 0)
    for t in range(columns // tile):
        product(kv - 1, t)
        for other in range(n_heads):
            xsend[other, :, t * tile : (t + 1) * tile] = acc[
                other * out_rows : (other + 1) * out_rows, t * tile : (t + 1) * tile
            ].astype(jnp.bfloat16)
        for step in range(1, n_heads):
            x_copy(t, lax.rem(x + step, n_heads)).start()
    for t in range(columns // tile):
        cols = slice(t * tile, (t + 1) * tile)
        total = acc[pl.ds(pl.multiple_of(x * out_rows, out_rows), out_rows), cols]
        for step in range(1, n_heads):
            other = lax.rem(x + step, n_heads)
            x_arrival(t, other).wait_recv()
            total = total + xrecv[other, :, cols].astype(jnp.float32)
        out_ref[:, cols] = total.astype(jnp.bfloat16)

    for step in range(1, n_ctx):
        lim_copy(z, lax.rem(z + step, n_ctx)).wait_send()

    def drain(k, carry):
        def each(s, inner):
            @pl.when(s != z)
            def _():
                p_copy(k, s).wait_send()
                s_copy(k, s).wait_send()

            @pl.when(jnp.logical_and(right, s <= z))
            def _():
                q_copy(k, s, 0).wait_send()
                a_copy(k, s, 0).wait_send()

            @pl.when(jnp.logical_and(left, s >= z))
            def _():
                q_copy(k, s, 1).wait_send()
                a_copy(k, s, 1).wait_send()

            for step in range(1, n_rep):
                c_copy(k, s, step).wait_send()
            return inner

        return lax.fori_loop(0, n_ctx, each, carry)

    lax.fori_loop(0, kv, drain, 0)
    for t in range(columns // tile):
        for step in range(1, n_heads):
            x_copy(t, lax.rem(x + step, n_heads)).wait_send()


def local(mesh_shape, queries, cache_keys, cache_values, new_keys, new_values, positions, cached_length, out_weight):
    rows, local_heads, head = queries.shape
    block, kv = cache_keys.shape[0], cache_keys.shape[1]
    per_group = local_heads // kv
    n_ctx, n_rep, n_heads = mesh_shape["ctx"], mesh_shape["rep"], mesh_shape["heads"]
    lanes = per_group * rows
    depth = per_group * head
    columns = out_weight.shape[1]
    tile = min(512, columns)
    tokens = n_ctx * n_rep * rows
    out_rows = tokens // n_heads

    sizes = (n_ctx, n_rep, n_heads, kv, rows, per_group, head, block)
    dma = pltpu.SemaphoreType.DMA
    vmem = pl.BlockSpec(memory_space=pltpu.VMEM)
    smem = pl.BlockSpec(memory_space=pltpu.SMEM)
    anywhere = pl.BlockSpec(memory_space=pl.ANY)
    return pl.pallas_call(
        functools.partial(kernel, sizes),
        out_shape=jax.ShapeDtypeStruct((out_rows, columns), jnp.bfloat16),
        in_specs=[smem, smem, vmem, anywhere, anywhere, vmem, vmem, anywhere],
        out_specs=vmem,
        scratch_shapes=[
            pltpu.VMEM((max(rows * local_heads, min(256, block) * kv), head), jnp.float32),
            pltpu.VMEM((block * kv, head), jnp.bfloat16),
            pltpu.VMEM((block * kv, head), jnp.bfloat16),
            pltpu.VMEM((kv, block, head), jnp.bfloat16),
            pltpu.VMEM((kv, head, block), jnp.bfloat16),
            pltpu.VMEM((kv, n_ctx, lanes, head), jnp.bfloat16),
            pltpu.VMEM((n_ctx, 1, lanes), jnp.int32),
            pltpu.VMEM((block, lanes), jnp.float32),
            pltpu.VMEM((kv, n_ctx, head, lanes), jnp.bfloat16),
            pltpu.VMEM((kv, n_ctx, head, lanes), jnp.bfloat16),
            pltpu.VMEM((kv, n_ctx, 2, lanes), jnp.float32),
            pltpu.VMEM((kv, n_ctx, 2, lanes), jnp.float32),
            pltpu.VMEM((kv, n_ctx, n_rep, rows, depth), jnp.bfloat16),
            pltpu.VMEM((tokens, columns), jnp.float32),
            pltpu.VMEM((n_heads, out_rows, columns), jnp.bfloat16),
            pltpu.VMEM((n_heads, out_rows, columns), jnp.bfloat16),
            pltpu.VMEM((kv, depth, columns), jnp.bfloat16),
            dma((kv, n_ctx, 2)),
            dma((kv, n_ctx)),
            dma((n_ctx,)),
            dma((n_ctx,)),
            dma((kv, n_ctx)),
            dma((kv, n_ctx)),
            dma((kv, n_ctx)),
            dma((kv, n_ctx)),
            dma((kv, n_ctx, 2)),
            dma((kv, n_ctx)),
            dma((kv, n_ctx, n_rep)),
            dma((kv, n_ctx, n_rep)),
            dma((columns // tile, n_heads)),
            dma((columns // tile, n_heads)),
            dma((kv,)),
            dma((2,)),
        ],
        compiler_params=pltpu.CompilerParams(
            collective_id=0, has_side_effects=True, vmem_limit_bytes=60 * 1024 * 1024
        ),
    )(
        positions,
        cached_length,
        queries.reshape(rows * local_heads, head),
        cache_keys.reshape(block * kv, head),
        cache_values.reshape(block * kv, head),
        new_keys.reshape(rows * kv, head),
        new_values.reshape(rows * kv, head),
        out_weight,
    )


def solution(mesh):
    return jax.shard_map(
        functools.partial(local, dict(mesh.shape)),
        mesh=mesh,
        in_specs=(
            P(("groups", "ctx", "rep"), "heads", None),
            P(("groups", "ctx"), "heads", None),
            P(("groups", "ctx"), "heads", None),
            P(("groups", "ctx", "rep"), "heads", None),
            P(("groups", "ctx", "rep"), "heads", None),
            P(("groups", "ctx", "rep")),
            P("groups"),
            P("heads", ("ctx", "rep")),
        ),
        out_specs=P(("groups", "heads"), ("ctx", "rep")),
        check_vma=False,
    )
```

```python
import functools

import jax
import jax.numpy as jnp
from jax import lax
from jax.experimental import pallas as pl
from jax.experimental.pallas import tpu as pltpu
from jax.sharding import PartitionSpec as P

MASKED = -1e30
FLOOR = -1e29
LOG2E = 1.4426950408889634
MESH = pl.DeviceIdType.MESH
NT = (((1,), (1,)), ((), ()))


def kernel(
    sizes, pos_ref, len_ref, q_ref, ck_ref, cv_ref, nk_ref, nv_ref, w_ref, out_ref,
    wide, kraw, vraw, key_ref, val_ref, qg, limg, scores, psend, precv, ssend, srecv, pown, ptmp, stmp, att, acc, xsend, xrecv, wbuf,
    q_ss, q_rs, l_ss, l_rs, p_ss, p_rs, s_ss, s_rs, a_ss, a_rs, c_ss, c_rs, x_ss, x_rs, w_sem, kv_sem, t_rs, u_rs,
):
    n_ctx, n_rep, n_heads, kv, rows, per_group, head, block = sizes
    z, r, x = lax.axis_index("ctx"), lax.axis_index("rep"), lax.axis_index("heads")
    lanes = per_group * rows
    factor = head ** (-0.5) * LOG2E
    piece = min(512, block)
    depth = per_group * head
    columns = w_ref.shape[1]
    tile = min(512, columns)
    out_rows = out_ref.shape[0]

    def w_copy(k):
        return pltpu.make_async_copy(w_ref.at[pl.ds(pl.multiple_of(k * depth, depth), depth), :], wbuf.at[k], w_sem.at[k])

    def remote(src, dst, send, recv, **where):
        return pltpu.make_async_remote_copy(
            src_ref=src, dst_ref=dst, send_sem=send, recv_sem=recv, device_id=where, device_id_type=MESH
        )

    def q_copy(k, s, way):
        return remote(qg.at[k, s], qg.at[k, s], q_ss.at[k, s, way], q_rs.at[k, s], ctx=z + 1 - 2 * way)

    def lim_copy(s, d):
        return remote(limg.at[s], limg.at[s], l_ss.at[d], l_rs.at[s], ctx=d)

    def p_copy(k, s):
        return remote(psend.at[k, s], precv.at[k, z], p_ss.at[k, s], p_rs.at[k, z], ctx=s)

    def p_arrival(k, s):
        return remote(psend.at[k, s], precv.at[k, s], p_ss.at[k, s], p_rs.at[k, s], ctx=s)

    def s_copy(k, s):
        return remote(ssend.at[k, s], srecv.at[k, z], s_ss.at[k, s], s_rs.at[k, z], ctx=s)

    def s_arrival(k, s):
        return remote(ssend.at[k, s], srecv.at[k, s], s_ss.at[k, s], s_rs.at[k, s], ctx=s)

    pair = z // 2
    partner = z + 1 - 2 * lax.rem(z, 2)

    def t_copy(k, s):
        return remote(psend.at[k, s], ptmp.at[k, s], p_ss.at[k, s], t_rs.at[k, s], ctx=partner)

    def u_copy(k, s):
        return remote(ssend.at[k, s], stmp.at[k, s], s_ss.at[k, s], u_rs.at[k, s], ctx=partner)

    def nearer(s):
        return jnp.where(s > z, lax.rem(z, 2) == 1, lax.rem(z, 2) == 0)

    def a_copy(k, s, way):
        return remote(att.at[k, s, r], att.at[k, s, r], a_ss.at[k, s, way], a_rs.at[k, s], ctx=z + 1 - 2 * way)

    def c_copy(k, s, step):
        other = lax.rem(r + step, n_rep)
        return remote(att.at[k, s, r], att.at[k, s, r], c_ss.at[k, s, step - 1], c_rs.at[k, s, r], rep=other)

    def c_arrival(k, s, step):
        other = lax.rem(r + step, n_rep)
        return remote(att.at[k, s, other], att.at[k, s, other], c_ss.at[k, s, step - 1], c_rs.at[k, s, other], rep=other)

    def x_copy(t, other):
        cols = pl.ds(t * tile, tile)
        return remote(xsend.at[other, :, cols], xrecv.at[x, :, cols], x_ss.at[t, other], x_rs.at[t, x], heads=other)

    def x_arrival(t, other):
        cols = pl.ds(t * tile, tile)
        return remote(xsend.at[other, :, cols], xrecv.at[other, :, cols], x_ss.at[t, other], x_rs.at[t, other], heads=other)

    k_copy = pltpu.make_async_copy(ck_ref, kraw, kv_sem.at[0])
    v_copy = pltpu.make_async_copy(cv_ref, vraw, kv_sem.at[1])
    k_copy.start()
    v_copy.start()
    for k in range(kv):
        w_copy(k).start()

    barrier = pltpu.get_barrier_semaphore()
    for step in range(1, n_ctx):
        pl.semaphore_signal(barrier, inc=1, device_id={"ctx": lax.rem(z + step, n_ctx)}, device_id_type=MESH)
    for step in range(1, n_rep):
        pl.semaphore_signal(barrier, inc=1, device_id={"rep": lax.rem(r + step, n_rep)}, device_id_type=MESH)
    for step in range(1, n_heads):
        pl.semaphore_signal(barrier, inc=1, device_id={"heads": lax.rem(x + step, n_heads)}, device_id_type=MESH)
    heads_here = kv * per_group
    wide[: rows * heads_here, :] = q_ref[...].astype(jnp.float32)
    for k in range(kv):
        for h in range(per_group):
            picked = wide[pl.ds(k * per_group + h, rows, stride=heads_here), :]
            qg[k, z, h * rows : (h + 1) * rows, :] = picked.astype(jnp.bfloat16)
    lane_token = lax.rem(lax.broadcasted_iota(jnp.int32, (1, lanes), 1), rows)
    limit_row = jnp.zeros((1, lanes), jnp.int32)
    for t in range(rows):
        limit_row = jnp.where(lane_token == t, jnp.minimum(len_ref[0], pos_ref[t]), limit_row)
    limg[z] = limit_row
    pl.semaphore_wait(barrier, n_ctx + n_rep + n_heads - 3)

    right, left = z < n_ctx - 1, z > 0

    def send_own(k):
        @pl.when(right)
        def _():
            q_copy(k, z, 0).start()

        @pl.when(left)
        def _():
            q_copy(k, z, 1).start()

    for k in range(min(2, kv)):
        send_own(k)
    for step in range(1, n_ctx):
        lim_copy(z, lax.rem(z + step, n_ctx)).start()

    batch = min(256, block)

    def unpack(c, carry):
        source = pl.ds(pl.multiple_of(c * batch * kv, batch * kv), batch * kv)
        span = pl.ds(pl.multiple_of(c * batch, batch), batch)
        wide[: batch * kv, :] = kraw[source, :].astype(jnp.float32)
        for k in range(kv):
            key_ref[k, span, :] = wide[pl.ds(k, batch, stride=kv), :].astype(jnp.bfloat16)
        return carry

    def unpack_values(c, carry):
        source = pl.ds(pl.multiple_of(c * batch * kv, batch * kv), batch * kv)
        span = pl.ds(pl.multiple_of(c * batch, batch), batch)
        wide[: batch * kv, :] = vraw[source, :].astype(jnp.float32)
        for k in range(kv):
            val_ref[k, :, span] = jnp.transpose(wide[pl.ds(k, batch, stride=kv), :]).astype(jnp.bfloat16)
        return carry

    k_copy.wait()
    lax.fori_loop(0, block // batch, unpack, 0)
    v_copy.wait()
    lax.fori_loop(0, block // batch, unpack_values, 0)

    def attend(k, s):
        query = qg[k, s]
        limit = limg[s] - z * block
        peak = jnp.full((1, lanes), FLOOR, jnp.float32)
        for c in range(block // piece):
            span = slice(c * piece, (c + 1) * piece)
            raw = lax.dot_general(key_ref[k, span, :], query, NT, preferred_element_type=jnp.float32)
            slot = lax.broadcasted_iota(jnp.int32, (piece, lanes), 0) + c * piece
            raw = jnp.where(slot < limit, raw, MASKED)
            scores[span, :] = raw
            peak = jnp.maximum(peak, jnp.max(raw, axis=0, keepdims=True))
        total = jnp.zeros((1, lanes), jnp.float32)
        output = jnp.zeros((head, lanes), jnp.float32)
        for c in range(block // piece):
            span = slice(c * piece, (c + 1) * piece)
            weights = jnp.exp2((scores[span, :] - peak) * factor)
            total = total + jnp.sum(weights, axis=0, keepdims=True)
            output = output + jnp.dot(val_ref[k, :, span], weights.astype(jnp.bfloat16), preferred_element_type=jnp.float32)

        @pl.when(s == z)
        def _():
            precv[k, z] = output.astype(jnp.bfloat16)
            srecv[k, z, 0:1, :] = peak
            srecv[k, z, 1:2, :] = total

        inside = s // 2 == pair

        @pl.when(s != z)
        def _():
            ssend[k, s, 0:1, :] = peak
            ssend[k, s, 1:2, :] = total

        @pl.when(jnp.logical_and(s != z, jnp.logical_or(inside, jnp.logical_not(nearer(s)))))
        def _():
            psend[k, s] = output.astype(jnp.bfloat16)

        @pl.when(jnp.logical_and(s != z, inside))
        def _():
            p_copy(k, s).start()
            s_copy(k, s).start()

        @pl.when(jnp.logical_and(jnp.logical_not(inside), jnp.logical_not(nearer(s))))
        def _():
            t_copy(k, s).start()
            u_copy(k, s).start()

        @pl.when(jnp.logical_and(jnp.logical_not(inside), nearer(s)))
        def _():
            pown[lax.rem(k, 2), s] = output

    def forward(k):
        def each(s, carry):
            @pl.when(jnp.logical_and(s // 2 != pair, nearer(s)))
            def _():
                t_copy(k, s).wait_recv()
                u_copy(k, s).wait_recv()
                mine, theirs = ssend[k, s, 0:1, :], stmp[k, s, 0:1, :]
                top = jnp.maximum(mine, theirs)
                mine, theirs = jnp.exp2((mine - top) * factor), jnp.exp2((theirs - top) * factor)
                total = mine * ssend[k, s, 1:2, :] + theirs * stmp[k, s, 1:2, :]
                output = mine * pown[lax.rem(k, 2), s] + theirs * ptmp[k, s].astype(jnp.float32)
                psend[k, s] = output.astype(jnp.bfloat16)
                ssend[k, s, 0:1, :] = top
                ssend[k, s, 1:2, :] = total
                p_copy(k, s).start()
                s_copy(k, s).start()

            return carry

        lax.fori_loop(0, n_ctx, each, 0)

    def q_hop(k, i):
        @pl.when(z - i >= 0)
        def _():
            q_copy(k, z - i, 0).wait_recv()

            @pl.when(right)
            def _():
                q_copy(k, z - i, 0).start()

            @pl.when(k == 0)
            def _():
                lim_copy(z - i, z - i).wait_recv()

        @pl.when(z + i < n_ctx)
        def _():
            q_copy(k, z + i, 1).wait_recv()

            @pl.when(left)
            def _():
                q_copy(k, z + i, 1).start()

            @pl.when(k == 0)
            def _():
                lim_copy(z + i, z + i).wait_recv()

    def visit(k, i):
        def side(j, inner):
            s = z - i + 2 * i * j
            real = jnp.logical_and(s >= 0, s < n_ctx)

            @pl.when(jnp.logical_and(real, jnp.logical_or(i > 0, j == 0)))
            def _():
                attend(k, s)

            return inner

        lax.fori_loop(0, 2, side, 0)

    def merge(k):
        sources = []
        for b in range(n_ctx // 2):
            s = jnp.where(b < pair, 2 * b + 1, jnp.where(b > pair, 2 * b, partner))
            p_arrival(k, s).wait_recv()
            s_arrival(k, s).wait_recv()
            sources.append(s)
        sources.append(z)
        query = qg[k, z]
        wide[: rows * kv, :] = nk_ref[...].astype(jnp.float32)
        own_key = wide[pl.ds(k, rows, stride=kv), :].astype(jnp.bfloat16)
        own_all = lax.dot_general(own_key, query, NT, preferred_element_type=jnp.float32)
        token = lax.rem(lax.broadcasted_iota(jnp.int32, (rows, lanes), 1), rows)
        same = token == lax.broadcasted_iota(jnp.int32, (rows, lanes), 0)
        own = jnp.sum(jnp.where(same, own_all, 0.0), axis=0, keepdims=True)
        wide[: rows * kv, :] = nv_ref[...].astype(jnp.float32)
        own_value = lax.dot_general(
            wide[pl.ds(k, rows, stride=kv), :].astype(jnp.bfloat16),
            jnp.where(same, 1.0, 0.0).astype(jnp.bfloat16),
            (((0,), (0,)), ((), ())),
            preferred_element_type=jnp.float32,
        )
        top = own
        for b in sources:
            top = jnp.maximum(top, srecv[k, b, 0:1, :])
        share = jnp.exp2((own - top) * factor)
        below = share
        above = share * own_value
        for b in sources:
            share = jnp.exp2((srecv[k, b, 0:1, :] - top) * factor)
            below = below + share * srecv[k, b, 1:2, :]
            above = above + share * precv[k, b].astype(jnp.float32)
        result = jnp.transpose(above / below).astype(jnp.bfloat16)
        for h in range(per_group):
            att[k, z, r, :, h * head : (h + 1) * head] = result[h * rows : (h + 1) * rows, :]

        @pl.when(right)
        def _():
            a_copy(k, z, 0).start()

        @pl.when(left)
        def _():
            a_copy(k, z, 1).start()

        for step in range(1, n_rep):
            c_copy(k, z, step).start()

    def a_hop(k, i):
        @pl.when(z - i >= 0)
        def _():
            a_copy(k, z - i, 0).wait_recv()

            @pl.when(right)
            def _():
                a_copy(k, z - i, 0).start()

            for step in range(1, n_rep):
                c_copy(k, z - i, step).start()

        @pl.when(z + i < n_ctx)
        def _():
            a_copy(k, z + i, 1).wait_recv()

            @pl.when(left)
            def _():
                a_copy(k, z + i, 1).start()

            for step in range(1, n_rep):
                c_copy(k, z + i, step).start()

    def gathered(k):
        for step in range(1, n_rep):
            for s in range(n_ctx):
                c_arrival(k, s, step).wait_recv()
        w_copy(k).wait()

    def product(k, t):
        cols = pl.ds(pl.multiple_of(t * tile, tile), tile)
        term = jnp.dot(
            att[k].reshape(n_ctx * n_rep * rows, depth), wbuf[k, :, cols], preferred_element_type=jnp.float32
        )
        acc[:, cols] += term

    acc[...] = jnp.zeros_like(acc)

    def stage(k, carry):
        @pl.when(k + 2 < kv)
        def _():
            send_own(k + 2)

        def step_of(i, inner):
            @pl.when(jnp.logical_and(k < kv, i > 0))
            def _():
                q_hop(k, i)

            @pl.when(jnp.logical_and(k >= 2, i > 0))
            def _():
                a_hop(k - 2, i)

            @pl.when(jnp.logical_and(jnp.logical_and(k >= 1, k <= kv), i == 1))
            def _():
                forward(k - 1)

            @pl.when(jnp.logical_and(jnp.logical_and(k >= 1, k <= kv), i == n_ctx - 1))
            def _():
                merge(k - 1)

            @pl.when(k < kv)
            def _():
                visit(k, i)

            return inner

        lax.fori_loop(0, n_ctx, step_of, 0)

        @pl.when(k >= 2)
        def _():
            gathered(k - 2)

        @pl.when(jnp.logical_and(k >= 2, k <= kv))
        def _():
            lax.fori_loop(0, columns // tile, lambda t, c: (product(k - 2, t), c)[1], 0)

        return carry

    lax.fori_loop(0, kv + 2, stage, 0)
    for t in range(columns // tile):
        product(kv - 1, t)
        for other in range(n_heads):
            xsend[other, :, t * tile : (t + 1) * tile] = acc[
                other * out_rows : (other + 1) * out_rows, t * tile : (t + 1) * tile
            ].astype(jnp.bfloat16)
        for step in range(1, n_heads):
            x_copy(t, lax.rem(x + step, n_heads)).start()
    for t in range(columns // tile):
        cols = slice(t * tile, (t + 1) * tile)
        total = acc[pl.ds(pl.multiple_of(x * out_rows, out_rows), out_rows), cols]
        for step in range(1, n_heads):
            other = lax.rem(x + step, n_heads)
            x_arrival(t, other).wait_recv()
            total = total + xrecv[other, :, cols].astype(jnp.float32)
        out_ref[:, cols] = total.astype(jnp.bfloat16)

    for step in range(1, n_ctx):
        lim_copy(z, lax.rem(z + step, n_ctx)).wait_send()

    def drain(k, carry):
        def each(s, inner):
            @pl.when(s != z)
            def _():
                p_copy(k, s).wait_send()
                s_copy(k, s).wait_send()

            @pl.when(jnp.logical_and(right, s <= z))
            def _():
                q_copy(k, s, 0).wait_send()
                a_copy(k, s, 0).wait_send()

            @pl.when(jnp.logical_and(left, s >= z))
            def _():
                q_copy(k, s, 1).wait_send()
                a_copy(k, s, 1).wait_send()

            for step in range(1, n_rep):
                c_copy(k, s, step).wait_send()
            return inner

        return lax.fori_loop(0, n_ctx, each, carry)

    lax.fori_loop(0, kv, drain, 0)
    for t in range(columns // tile):
        for step in range(1, n_heads):
            x_copy(t, lax.rem(x + step, n_heads)).wait_send()


def local(mesh_shape, queries, cache_keys, cache_values, new_keys, new_values, positions, cached_length, out_weight):
    rows, local_heads, head = queries.shape
    block, kv = cache_keys.shape[0], cache_keys.shape[1]
    per_group = local_heads // kv
    n_ctx, n_rep, n_heads = mesh_shape["ctx"], mesh_shape["rep"], mesh_shape["heads"]
    lanes = per_group * rows
    depth = per_group * head
    columns = out_weight.shape[1]
    tile = min(512, columns)
    tokens = n_ctx * n_rep * rows
    out_rows = tokens // n_heads

    sizes = (n_ctx, n_rep, n_heads, kv, rows, per_group, head, block)
    dma = pltpu.SemaphoreType.DMA
    vmem = pl.BlockSpec(memory_space=pltpu.VMEM)
    smem = pl.BlockSpec(memory_space=pltpu.SMEM)
    anywhere = pl.BlockSpec(memory_space=pl.ANY)
    return pl.pallas_call(
        functools.partial(kernel, sizes),
        out_shape=jax.ShapeDtypeStruct((out_rows, columns), jnp.bfloat16),
        in_specs=[smem, smem, vmem, anywhere, anywhere, vmem, vmem, anywhere],
        out_specs=vmem,
        scratch_shapes=[
            pltpu.VMEM((max(rows * local_heads, min(256, block) * kv), head), jnp.float32),
            pltpu.VMEM((block * kv, head), jnp.bfloat16),
            pltpu.VMEM((block * kv, head), jnp.bfloat16),
            pltpu.VMEM((kv, block, head), jnp.bfloat16),
            pltpu.VMEM((kv, head, block), jnp.bfloat16),
            pltpu.VMEM((kv, n_ctx, lanes, head), jnp.bfloat16),
            pltpu.VMEM((n_ctx, 1, lanes), jnp.int32),
            pltpu.VMEM((block, lanes), jnp.float32),
            pltpu.VMEM((kv, n_ctx, head, lanes), jnp.bfloat16),
            pltpu.VMEM((kv, n_ctx, head, lanes), jnp.bfloat16),
            pltpu.VMEM((kv, n_ctx, 2, lanes), jnp.float32),
            pltpu.VMEM((kv, n_ctx, 2, lanes), jnp.float32),
            pltpu.VMEM((2, n_ctx, head, lanes), jnp.float32),
            pltpu.VMEM((kv, n_ctx, head, lanes), jnp.bfloat16),
            pltpu.VMEM((kv, n_ctx, 2, lanes), jnp.float32),
            pltpu.VMEM((kv, n_ctx, n_rep, rows, depth), jnp.bfloat16),
            pltpu.VMEM((tokens, columns), jnp.float32),
            pltpu.VMEM((n_heads, out_rows, columns), jnp.bfloat16),
            pltpu.VMEM((n_heads, out_rows, columns), jnp.bfloat16),
            pltpu.VMEM((kv, depth, columns), jnp.bfloat16),
            dma((kv, n_ctx, 2)),
            dma((kv, n_ctx)),
            dma((n_ctx,)),
            dma((n_ctx,)),
            dma((kv, n_ctx)),
            dma((kv, n_ctx)),
            dma((kv, n_ctx)),
            dma((kv, n_ctx)),
            dma((kv, n_ctx, 2)),
            dma((kv, n_ctx)),
            dma((kv, n_ctx, n_rep)),
            dma((kv, n_ctx, n_rep)),
            dma((columns // tile, n_heads)),
            dma((columns // tile, n_heads)),
            dma((kv,)),
            dma((2,)),
            dma((kv, n_ctx)),
            dma((kv, n_ctx)),
        ],
        compiler_params=pltpu.CompilerParams(
            collective_id=0, has_side_effects=True, vmem_limit_bytes=60 * 1024 * 1024
        ),
    )(
        positions,
        cached_length,
        queries.reshape(rows * local_heads, head),
        cache_keys.reshape(block * kv, head),
        cache_values.reshape(block * kv, head),
        new_keys.reshape(rows * kv, head),
        new_values.reshape(rows * kv, head),
        out_weight,
    )


def solution(mesh):
    return jax.shard_map(
        functools.partial(local, dict(mesh.shape)),
        mesh=mesh,
        in_specs=(
            P(("groups", "ctx", "rep"), "heads", None),
            P(("groups", "ctx"), "heads", None),
            P(("groups", "ctx"), "heads", None),
            P(("groups", "ctx", "rep"), "heads", None),
            P(("groups", "ctx", "rep"), "heads", None),
            P(("groups", "ctx", "rep")),
            P("groups"),
            P("heads", ("ctx", "rep")),
        ),
        out_specs=P(("groups", "heads"), ("ctx", "rep")),
        check_vma=False,
    )
```
